32 devices in a mesh: group: 2 (over y), expert: 4 (over z), row: 2 (over x), col: 2 (over core).
Axes of the slice: x: 2, y: 2, z: 4, core: 2. Of those that a mesh axis runs over, the one named last changes fastest.
Arguments:
- tokens: bfloat16 [2048, 2048], P(('group', 'expert', 'row'), 'col'), parts along dimension 0, may hold values from -6 to 6
- expert_ids: int32 [2048, 2], P(('group', 'expert', 'row')), parts along dimension 0, may hold values from 0 to 3, as said below
- slot_ids: int32 [2048, 2], P(('group', 'expert', 'row')), parts along dimension 0, may hold values from 0 to 63, as said below
- gate_weights: float32 [2048, 2], P(('group', 'expert', 'row')), parts along dimension 0, may hold values from 0.2 to 1
- w_gate: bfloat16 [4, 2048, 1024], P('expert', 'col', 'row'), may hold values from -0.125 to 0.125
- w_up: bfloat16 [4, 2048, 1024], P('expert', 'col', 'row'), may hold values from -0.125 to 0.125
- w_down: bfloat16 [4, 1024, 2048], P('expert', 'row', 'col'), may hold values from -0.1875 to 0.1875
Outputs:
- combined: bfloat16 [2048, 2048], P(('group', 'expert', 'row'), 'col'), parts along dimension 0
The draws below stay inside these ranges and needn't reach their ends.
There are 2 independent parts, one for each index of `group`. The reference program is written for one: setup_inputs(seed, part) draws one part's arguments, and reference() takes and returns one part's arrays. A program takes and returns all parts, laid end to end along the dimension named above; an argument that names none is the same for every part. Nothing has to cross between parts.
Inputs may be any that keep to these rules, and one draw needn't show every extreme that they name: `expert_ids`: A row's two ids differ; within each aligned block of 128 rows (the rows of one device) every expert is named by exactly 64 of the block's 2 * 128 entries. `slot_ids`: within each aligned block of 128 rows, the entries that name one expert carry distinct slots.
All inputs are finite; a program needn't handle non-finite values.
Results may differ from the reference program's by a relative error of at most 0.0066.
Values may be sent and summed in bfloat16 or wider, within the bound.
No kernel may reach another device: no remote copies, remote signals or barrier semaphores. Data moves between devices by JAX's collectives and lax.ppermute only.
A program may use at most 64 MiB of HBM per device.

```python
import jax
import jax.numpy as jnp
from jax import lax

D = 2048
FF_WIN = 1024
TOK_DEV = 128
FF_DEV = 512
EXPERTS = 4
CAP = 64
TOKENS = 1024
N_ROW = 2


def route_table(key):
    blocks = TOKENS // TOK_DEV
    block_keys = jax.random.split(jax.random.fold_in(key, 11), blocks)

    def order_one(block_key):
        return jax.random.permutation(block_key, TOK_DEV).astype(jnp.int32)
    orders = jax.vmap(order_one)(block_keys)
    shifts = jax.random.randint(jax.random.fold_in(key, 13), (blocks, 1), 1, EXPERTS).astype(jnp.int32)
    primary = orders % EXPERTS
    secondary = (primary + shifts) % EXPERTS
    half_slots = TOK_DEV // EXPERTS
    slot_one = orders // EXPERTS
    slot_two = half_slots + slot_one
    experts_out = jnp.stack([primary.reshape(-1), secondary.reshape(-1)], axis=1).astype(jnp.int32)
    slots_out = jnp.stack([slot_one.reshape(-1), slot_two.reshape(-1)], axis=1).astype(jnp.int32)
    return (experts_out, slots_out)


def draw_expert_ids(key, part):
    return route_table(key)[0]


def draw_slot_ids(key, part):
    return route_table(key)[1]


def levels(own_key, shape, cuts, least, top_value):
    factor_of = 1.0
    for axis_at, shards_of in cuts:
        steps = jax.random.uniform(jax.random.fold_in(jax.random.fold_in(own_key, 6), axis_at), (shards_of,), jnp.float32, least / len(cuts), top_value / len(cuts))
        factor_of = factor_of * jnp.repeat(jnp.exp(steps), shape[axis_at] // shards_of).reshape((-1,) + (1,) * (len(shape) - 1 - axis_at))
    return factor_of


def scatter_about(stream_key, shape, deviation, reach, cuts=(), kind=jnp.bfloat16):
    drawn = deviation * jax.random.normal(stream_key, shape, jnp.float32)
    if cuts:
        drawn = drawn * levels(stream_key, shape, cuts, -0.22, 0.18)
    return jnp.clip(drawn, -reach, reach).astype(kind)


def setup_inputs(seed: int = 0, part: int = 0) -> dict:
    keys = jax.random.split(jax.random.key(seed), 8)
    part_splits = jax.random.split(jax.random.fold_in(keys[7], part), 8)
    return {
        "tokens": scatter_about(part_splits[0], (TOKENS, D), 1.0, 6.0, ((0, 8), (1, 2))),
        "expert_ids": draw_expert_ids(jax.random.fold_in(jax.random.fold_in(keys[7], part), 71), part),
        "slot_ids": draw_slot_ids(jax.random.fold_in(jax.random.fold_in(keys[7], part), 71), part),
        "gate_weights": jnp.clip(0.2 + 0.8 * jax.random.uniform(part_splits[3], (TOKENS, 2), jnp.float32) ** levels(part_splits[3], (TOKENS, 2), ((0, 8),), -0.2, 0.2), 0.2, 1.0),
        "w_gate": scatter_about(keys[4], (EXPERTS, D, FF_WIN), D ** -0.5, 0.125, ((0, 4), (1, 2), (2, 2))),
        "w_up": scatter_about(keys[5], (EXPERTS, D, FF_WIN), D ** -0.5, 0.125, ((0, 4), (1, 2), (2, 2))),
        "w_down": scatter_about(keys[6], (EXPERTS, FF_WIN, D), FF_WIN ** -0.5, 0.1875, ((0, 4), (1, 2), (2, 2))),
    }


def reference(tokens, expert_ids, slot_ids, gate_weights, w_gate, w_up, w_down):
    rows_total = N_ROW * EXPERTS * CAP
    positions = jnp.arange(TOKENS, dtype=jnp.int32)
    source = positions // TOK_DEV
    src_expert = source // N_ROW
    src_row = source % N_ROW
    base_row = (src_row * EXPERTS + src_expert) * CAP
    dest_rows = (base_row[:, None] + slot_ids).astype(jnp.int32)
    flat_dest = (expert_ids * rows_total + dest_rows).astype(jnp.int32)
    dispatched = jnp.zeros((EXPERTS * rows_total, D), tokens.dtype)
    dispatched = dispatched.at[flat_dest[:, 0]].set(tokens).at[flat_dest[:, 1]].set(tokens)
    dispatched = dispatched.reshape(EXPERTS, rows_total, D)

    def expert_pass(operands):
        block, gate_w, up_w, down_w = operands
        gate_part = jnp.dot(block.astype(jnp.float32), gate_w.astype(jnp.float32), preferred_element_type=jnp.float32)
        up_part = jnp.dot(block.astype(jnp.float32), up_w.astype(jnp.float32), preferred_element_type=jnp.float32)
        hidden = lax.optimization_barrier((jax.nn.silu(gate_part) * up_part).astype(jnp.bfloat16))
        pieces = hidden.astype(jnp.float32).reshape(rows_total, N_ROW, FF_DEV)
        down_pieces = down_w.astype(jnp.float32).reshape(N_ROW, FF_DEV, D)
        partial_value = jnp.einsum('rnf,nfd->nrd', pieces, down_pieces)
        partial_value = lax.optimization_barrier(partial_value.astype(jnp.bfloat16))
        return jnp.sum(partial_value.astype(jnp.float32), axis=0).astype(jnp.bfloat16)

    outputs = lax.map(expert_pass, (dispatched, w_gate, w_up, w_down))
    flat_out = outputs.reshape(EXPERTS * rows_total, D).astype(jnp.float32)
    combined = gate_weights[:, 0:1] * flat_out[flat_dest[:, 0]] + gate_weights[:, 1:2] * flat_out[flat_dest[:, 1]]
    return combined.astype(jnp.bfloat16)
```

```python
import jax
import jax.numpy as jnp
from jax import lax
from jax.sharding import PartitionSpec as P


def partner(size, step, index):
    if size & (size - 1) == 0:
        return index ^ step
    return (index + step) % size


def send(block, axis, size, step, back=False):
    pairs = [(i, partner(size, step, i)) for i in range(size)]
    if back:
        pairs = [(b, a) for a, b in pairs]
    return lax.ppermute(block, axis, pairs)


def per_device(tokens, expert_ids, slot_ids, gate_weights, w_gate, w_up, w_down):
    experts = lax.axis_size("expert")
    rows = lax.axis_size("row")
    cols = lax.axis_size("col")
    mine = lax.axis_index("expert")
    tok_rows, width = tokens.shape
    capacity = 2 * tok_rows // experts
    hidden_cols = w_gate.shape[2]
    if experts & (experts - 1) == 0:
        relative = expert_ids ^ mine
    else:
        relative = (expert_ids - mine) % experts
    destination = relative * capacity + slot_ids
    places = jnp.arange(experts * capacity, dtype=jnp.int32)
    select = (
        (places[:, None] == destination[None, :, 0]) | (places[:, None] == destination[None, :, 1])
    ).astype(jnp.bfloat16)
    outbound = jnp.dot(select, tokens, preferred_element_type=jnp.float32).astype(jnp.bfloat16)
    outbound = outbound.reshape(experts, capacity, width)
    order = sorted(range(experts), key=lambda s: (s == 0, -s))
    arrived = {s: send(outbound[s], "expert", experts, s) if s else outbound[0] for s in order}
    blocks = {(s, 0): arrived[s] for s in order}
    for s in [0] + [s for s in order if s]:
        for j in range(1, rows):
            blocks[s, j] = send(arrived[s], "row", rows, j)
    keys = [(s, j) for s in range(experts) for j in range(rows)]
    gathered = jnp.concatenate([blocks[k] for k in keys], axis=0)
    joined = jnp.concatenate([w_gate[0], w_up[0]], axis=1)
    own = jnp.dot(gathered, joined, preferred_element_type=jnp.float32)
    summed = own
    for j in range(1, cols):
        summed = summed + send(own.astype(jnp.bfloat16), "col", cols, j).astype(jnp.float32)
    hidden = (jax.nn.silu(summed[:, :hidden_cols]) * summed[:, hidden_cols:]).astype(jnp.bfloat16)
    term = jnp.dot(hidden, w_down[0], preferred_element_type=jnp.float32).astype(jnp.bfloat16)
    term = term.reshape(experts, rows, capacity, width)
    returned = {}
    for s in order:
        total = term[s, 0].astype(jnp.float32)
        for j in range(1, rows):
            total = total + send(term[s, j], "row", rows, j, True).astype(jnp.float32)
        expert_out = total.astype(jnp.bfloat16)
        returned[s] = send(expert_out, "expert", experts, s, True) if s else expert_out
    returned = jnp.concatenate([returned[s] for s in range(experts)], axis=0)
    combined = 0.0
    for k in range(2):
        pick = (destination[:, k][:, None] == places[None, :]).astype(jnp.bfloat16)
        row = jnp.dot(pick, returned, preferred_element_type=jnp.float32)
        combined = combined + gate_weights[:, k : k + 1] * row
    return combined.astype(jnp.bfloat16)


def solution(mesh):
    return jax.shard_map(
        per_device,
        mesh=mesh,
        in_specs=(
            P(("group", "expert", "row"), "col"),
            P(("group", "expert", "row"), None),
            P(("group", "expert", "row"), None),
            P(("group", "expert", "row"), None),
            P("expert", "col", "row"),
            P("expert", "col", "row"),
            P("expert", "row", "col"),
        ),
        out_specs=P(("group", "expert", "row"), "col"),
        check_vma=False,
    )
```

```python
import jax
import jax.numpy as jnp
from jax import lax
from jax.experimental import pallas as pl
from jax.experimental.pallas import tpu as pltpu
from jax.sharding import PartitionSpec as P

LEAN = pltpu.CompilerParams(vmem_limit_bytes=8 << 20)
HBM = pl.BlockSpec(memory_space=pltpu.HBM)
VMEM = pl.BlockSpec(memory_space=pltpu.VMEM)

FINISH = (1, 2, 0, 3)
FLIP = False


def partner(size, step, index):
    if FLIP and size & (size - 1) == 0:
        return index ^ step
    return (index + step) % size


def send(block, axis, size, step, back=False):
    pairs = [(i, partner(size, step, i)) for i in range(size)]
    if back:
        pairs = [(b, a) for a, b in pairs]
    return lax.ppermute(block, axis, pairs)


def step_of(expert_ids, experts):
    mine = lax.axis_index("expert")
    if FLIP and experts & (experts - 1) == 0:
        return expert_ids ^ mine
    return lax.rem(expert_ids - mine + experts, experts)


def stay(*arrays):
    return [pltpu.with_memory_space_constraint(array, pltpu.HBM) for array in arrays]


def call(kernel, arrays, in_specs, out_shape, scratch=()):
    return pl.pallas_call(
        kernel,
        out_shape=out_shape,
        in_specs=in_specs,
        out_specs=jax.tree.map(lambda _: VMEM, out_shape),
        scratch_shapes=scratch,
        compiler_params=LEAN,
    )(*arrays)


def fetch(pairs, sems):
    copies = [pltpu.make_async_copy(src, dst, sems.at[i]) for i, (src, dst) in enumerate(pairs)]
    for copy in copies:
        copy.start()
    return copies


def select(tokens, expert_ids, slot_ids, gate_weights, experts, capacity):
    tok_rows, width = tokens.shape

    def kernel(ids_hbm, slots_hbm, weights_hbm, tokens_hbm, *refs):
        outs, (seat_ref, weight_ref, ids_ref, slots_ref, weights_ref, tokens_ref, sems) = refs[:experts], refs[experts:]
        copies = fetch(
            ((tokens_hbm, tokens_ref), (ids_hbm, ids_ref), (slots_hbm, slots_ref), (weights_hbm, weights_ref)), sems
        )
        for copy in copies[1:]:
            copy.wait()
        step = step_of(ids_ref[...], experts)
        slots = slots_ref[...]
        weights = weights_ref[...]
        picks = []
        for s in range(experts):
            mine = step == s
            seat = jnp.max(jnp.where(mine, slots, -1), axis=0, keepdims=True)
            seat_ref[s : s + 1, :] = seat
            weight_ref[s : s + 1, :] = jnp.sum(jnp.where(mine, weights, 0.0), axis=0, keepdims=True)
            seats = lax.broadcasted_iota(jnp.int32, (capacity, tok_rows), 0)
            picks.append(jnp.where(seats == seat, 1.0, 0.0).astype(jnp.bfloat16))
        copies[0].wait()
        rows = tokens_ref[...]
        for s, out in enumerate(outs):
            out[...] = jnp.dot(picks[s], rows, preferred_element_type=jnp.float32).astype(out.dtype)

    outs = call(
        kernel,
        stay(expert_ids.T, slot_ids.T, gate_weights.T, tokens),
        [HBM] * 4,
        [pltpu.VMEM((capacity, width), tokens.dtype)] * experts
        + [pltpu.VMEM((experts, tok_rows), jnp.int32), pltpu.VMEM((experts, tok_rows), jnp.float32)],
        [
            pltpu.VMEM((2, tok_rows), jnp.int32),
            pltpu.VMEM((2, tok_rows), jnp.int32),
            pltpu.VMEM((2, tok_rows), jnp.float32),
            pltpu.VMEM((tok_rows, width), tokens.dtype),
            pltpu.SemaphoreType.DMA((4,)),
        ],
    )
    return outs[:experts], outs[experts], outs[experts + 1]


def bring(*arrays):
    def kernel(*refs):
        n = len(arrays)
        for copy in fetch(zip(refs[:n], refs[n : 2 * n]), refs[-1]):
            copy.wait()

    return call(
        kernel,
        stay(*arrays),
        [HBM] * len(arrays),
        [pltpu.VMEM(array.shape, array.dtype) for array in arrays],
        [pltpu.SemaphoreType.DMA((len(arrays),))],
    )


def enter(blocks, gate, up):
    def kernel(*refs):
        *block_refs, gate_ref, up_ref, outgoing_ref, own_ref = refs
        gathered = jnp.concatenate([block[...] for block in block_refs], axis=0)
        cols = gate_ref.shape[1]
        for i, ref in enumerate((gate_ref, up_ref)):
            part = jnp.dot(gathered, ref[...], preferred_element_type=jnp.float32)
            own_ref[:, i * cols : (i + 1) * cols] = part
            outgoing_ref[:, i * cols : (i + 1) * cols] = part.astype(outgoing_ref.dtype)

    shape = (sum(block.shape[0] for block in blocks), 2 * gate.shape[1])
    arrays = (*blocks, gate, up)
    return call(kernel, arrays, [VMEM] * len(arrays), [pltpu.VMEM(shape, jnp.bfloat16), pltpu.VMEM(shape, jnp.float32)])


def leave(own, others, down, rows):
    def kernel(own_ref, *refs):
        summed = own_ref[...]
        cols = summed.shape[1] // 2
        for other in refs[: len(others)]:
            summed = summed + other[...].astype(jnp.float32)
        down_ref, *outs = refs[len(others) :]
        hidden = (jax.nn.silu(summed[:, :cols]) * summed[:, cols:]).astype(jnp.bfloat16)
        term = jnp.dot(hidden, down_ref[...], preferred_element_type=jnp.float32)
        for i, out in enumerate(outs):
            size = out.shape[0]
            out[...] = term[i * size : (i + 1) * size].astype(out.dtype)

    arrays = (own, *others, down)
    shape = (own.shape[0] // rows, down.shape[1])
    return call(kernel, arrays, [VMEM] * len(arrays), [pltpu.VMEM(shape, jnp.bfloat16)] * rows)


def combine(steps, blocks, seat, weight, total, out_shape):
    def kernel(*refs):
        block_refs, (seat_ref, weight_ref, *total_ref, out_ref) = refs[: len(steps)], refs[len(steps) :]
        capacity = block_refs[0].shape[0]
        tok_rows = seat_ref.shape[1]
        columns = jnp.transpose(
            jnp.concatenate([weight_ref[...]] * -(-8 // weight_ref.shape[0]), axis=0)
        )
        result = total_ref[0][...] if total_ref else 0.0
        for s, block in zip(steps, block_refs):
            seats = lax.broadcasted_iota(jnp.int32, (capacity, tok_rows), 0)
            pick = jnp.where(seats == seat_ref[s : s + 1, :], 1.0, 0.0).astype(jnp.bfloat16)
            rows = lax.dot_general(
                pick, block[...], (((0,), (0,)), ((), ())), preferred_element_type=jnp.float32
            )
            result = result + columns[:, s : s + 1] * rows
        out_ref[...] = result.astype(out_ref.dtype)

    arrays = (*blocks, seat, weight) + (() if total is None else (total,))
    return call(kernel, arrays, [VMEM] * len(arrays), out_shape)


def per_device(tokens, expert_ids, slot_ids, gate_weights, w_gate, w_up, w_down):
    experts = lax.axis_size("expert")
    rows = lax.axis_size("row")
    cols = lax.axis_size("col")
    capacity = 2 * tokens.shape[0] // experts
    outbound, seat, weight = select(tokens, expert_ids, slot_ids, gate_weights, experts, capacity)
    gate, up, down = bring(w_gate[0], w_up[0], w_down[0])
    returned = []
    for s in range(experts):
        arrived = send(outbound[s], "expert", experts, s) if s else outbound[0]
        blocks = [arrived] + [send(arrived, "row", rows, j) for j in range(1, rows)]
        outgoing, own = enter(blocks, gate, up)
        others = [send(outgoing, "col", cols, j) for j in range(1, cols)]
        term = leave(own, others, down, rows)
        others = [send(term[j], "row", rows, j, True) for j in range(1, rows)]
        total = sum([other.astype(jnp.float32) for other in others], term[0].astype(jnp.float32))
        expert_out = total.astype(jnp.bfloat16)
        returned.append(send(expert_out, "expert", experts, s, True) if s else expert_out)
    order = FINISH if experts == len(FINISH) else tuple(range(experts))
    early, last = order[:-1], order[-1:]
    partial = combine(early, [returned[s] for s in early], seat, weight, None, pltpu.VMEM(tokens.shape, jnp.float32))
    return combine(
        last, [returned[s] for s in last], seat, weight, partial, jax.ShapeDtypeStruct(tokens.shape, jnp.bfloat16)
    )


def solution(mesh):
    return jax.shard_map(
        per_device,
        mesh=mesh,
        in_specs=(
            P(("group", "expert", "row"), "col"),
            P(("group", "expert", "row"), None),
            P(("group", "expert", "row"), None),
            P(("group", "expert", "row"), None),
            P("expert", "col", "row"),
            P("expert", "col", "row"),
            P("expert", "row", "col"),
        ),
        out_specs=P(("group", "expert", "row"), "col"),
        check_vma=False,
    )
```

```python
import jax
import jax.numpy as jnp
from jax import lax
from jax.experimental import pallas as pl
from jax.experimental.pallas import tpu as pltpu
from jax.sharding import PartitionSpec as P

LEAN = pltpu.CompilerParams(vmem_limit_bytes=8 << 20)
HBM = pl.BlockSpec(memory_space=pltpu.HBM)
VMEM = pl.BlockSpec(memory_space=pltpu.VMEM)
LANES = 128

FINISH = (3, 2, 0, 1)
GRAY = True


def seat_in_ring(size, index):
    return index ^ (index >> 1) if GRAY and size == 4 else index


def partner(size, step, index):
    return seat_in_ring(size, (seat_in_ring(size, index) + step) % size)


def send(block, axis, size, step, back=False):
    pairs = [(i, partner(size, step, i)) for i in range(size)]
    if back:
        pairs = [(b, a) for a, b in pairs]
    return lax.ppermute(block, axis, pairs)


def step_of(expert_ids, experts):
    mine = seat_in_ring(experts, lax.axis_index("expert"))
    return lax.rem(seat_in_ring(experts, expert_ids) - mine + experts, experts)


def stay(*arrays):
    return [pltpu.with_memory_space_constraint(array, pltpu.HBM) for array in arrays]


def call(kernel, arrays, in_specs, out_shape, scratch=()):
    return pl.pallas_call(
        kernel,
        out_shape=out_shape,
        in_specs=in_specs,
        out_specs=jax.tree.map(lambda _: VMEM, out_shape),
        scratch_shapes=scratch,
        compiler_params=LEAN,
    )(*arrays)


def fetch(pairs, sems):
    copies = [pltpu.make_async_copy(src, dst, sems.at[i]) for i, (src, dst) in enumerate(pairs)]
    for copy in copies:
        copy.start()
    return copies


def select(tokens, expert_ids, slot_ids, gate_weights, experts, capacity):
    tok_rows, width = tokens.shape

    def kernel(ids_hbm, slots_hbm, weights_hbm, tokens_hbm, *refs):
        outs, (seat_ref, weight_ref, ids_ref, slots_ref, weights_ref, tokens_ref, sems) = refs[:experts], refs[experts:]
        copies = fetch(
            ((tokens_hbm, tokens_ref), (ids_hbm, ids_ref), (slots_hbm, slots_ref), (weights_hbm, weights_ref)), sems
        )
        for copy in copies[1:]:
            copy.wait()
        step = step_of(ids_ref[...], experts)
        slots = slots_ref[...]
        weights = weights_ref[...]
        picks = []
        for s in range(experts):
            mine = step == s
            seat = jnp.max(jnp.where(mine, slots, -1), axis=0, keepdims=True)
            seat_ref[s : s + 1, :] = seat
            weight_ref[s : s + 1, :] = jnp.sum(jnp.where(mine, weights, 0.0), axis=0, keepdims=True)
            seats = lax.broadcasted_iota(jnp.int32, (capacity, tok_rows), 0)
            picks.append(jnp.where(seats == seat, 1.0, 0.0).astype(jnp.bfloat16))
        copies[0].wait()
        rows = tokens_ref[...]
        for s, out in enumerate(outs):
            out[...] = jnp.dot(picks[s], rows, preferred_element_type=jnp.float32).astype(out.dtype)

    outs = call(
        kernel,
        stay(expert_ids.T, slot_ids.T, gate_weights.T, tokens),
        [HBM] * 4,
        [pltpu.VMEM((capacity, width), tokens.dtype)] * experts
        + [pltpu.VMEM((experts, tok_rows), jnp.int32), pltpu.VMEM((experts, tok_rows), jnp.float32)],
        [
            pltpu.VMEM((2, tok_rows), jnp.int32),
            pltpu.VMEM((2, tok_rows), jnp.int32),
            pltpu.VMEM((2, tok_rows), jnp.float32),
            pltpu.VMEM((tok_rows, width), tokens.dtype),
            pltpu.SemaphoreType.DMA((4,)),
        ],
    )
    return outs[:experts], outs[experts], outs[experts + 1]


def bring(*arrays):
    def kernel(*refs):
        n = len(arrays)
        for copy in fetch(zip(refs[:n], refs[n : 2 * n]), refs[-1]):
            copy.wait()

    return call(
        kernel,
        stay(*arrays),
        [HBM] * len(arrays),
        [pltpu.VMEM(array.shape, array.dtype) for array in arrays],
        [pltpu.SemaphoreType.DMA((len(arrays),))],
    )


def enter(blocks, gate, up):
    def kernel(*refs):
        *block_refs, gate_ref, up_ref, outgoing_ref, own_ref = refs
        gathered = jnp.concatenate([block[...] for block in block_refs], axis=0)
        cols = gate_ref.shape[1]
        for i, ref in enumerate((gate_ref, up_ref)):
            part = jnp.dot(gathered, ref[...], preferred_element_type=jnp.float32)
            own_ref[:, i * cols : (i + 1) * cols] = part
            outgoing_ref[:, i * cols : (i + 1) * cols] = part.astype(outgoing_ref.dtype)

    shape = (sum(block.shape[0] for block in blocks), 2 * gate.shape[1])
    arrays = (*blocks, gate, up)
    return call(kernel, arrays, [VMEM] * len(arrays), [pltpu.VMEM(shape, jnp.bfloat16), pltpu.VMEM(shape, jnp.float32)])


def leave(own, others, down, rows):
    def kernel(own_ref, *refs):
        summed = own_ref[...]
        cols = summed.shape[1] // 2
        for other in refs[: len(others)]:
            summed = summed + other[...].astype(jnp.float32)
        down_ref, *outs = refs[len(others) :]
        hidden = (jax.nn.silu(summed[:, :cols]) * summed[:, cols:]).astype(jnp.bfloat16)
        term = jnp.dot(hidden, down_ref[...], preferred_element_type=jnp.float32)
        for i, out in enumerate(outs):
            size = out.shape[0]
            out[...] = term[i * size : (i + 1) * size].astype(out.dtype)

    arrays = (own, *others, down)
    shape = (own.shape[0] // rows, down.shape[1])
    return call(kernel, arrays, [VMEM] * len(arrays), [pltpu.VMEM(shape, jnp.bfloat16)] * rows)


def picked(seat_ref, step, capacity):
    seats = lax.broadcasted_iota(jnp.int32, (capacity, seat_ref.shape[1]), 0)
    return jnp.where(seats == seat_ref[step : step + 1, :], 1.0, 0.0)


def combine_early(steps, last, blocks, seat, weight, width):
    def kernel(*refs):
        block_refs, (seat_ref, weight_ref, total_ref, pick_ref, column_ref) = refs[: len(steps)], refs[len(steps) :]
        columns = jnp.transpose(jnp.concatenate([weight_ref[...]] * -(-8 // weight_ref.shape[0]), axis=0))
        total = 0.0
        for s, block in zip(steps, block_refs):
            pick = picked(seat_ref, s, block.shape[0]).astype(jnp.bfloat16)
            rows = lax.dot_general(
                pick, block[...], (((0,), (0,)), ((), ())), preferred_element_type=jnp.float32
            )
            total = total + columns[:, s : s + 1] * rows
        total_ref[...] = total
        pick_ref[...] = jnp.transpose(picked(seat_ref, last, pick_ref.shape[1])).astype(jnp.bfloat16)
        column_ref[...] = jnp.broadcast_to(columns[:, last : last + 1], column_ref.shape)

    tok_rows = seat.shape[1]
    arrays = (*blocks, seat, weight)
    return call(
        kernel,
        arrays,
        [VMEM] * len(arrays),
        [
            pltpu.VMEM((tok_rows, width), jnp.float32),
            pltpu.VMEM((tok_rows, blocks[0].shape[0]), jnp.bfloat16),
            pltpu.VMEM((tok_rows, LANES), jnp.float32),
        ],
    )


def combine_last(block, total, pick, column):
    tok_rows, width = total.shape
    pieces = 4
    size = width // pieces

    def kernel(block_ref, total_ref, pick_ref, column_ref, out_hbm, out_ref, sems):
        scale = jnp.concatenate([column_ref[...]] * (size // LANES), axis=1)
        copies = []
        for i in range(pieces):
            part = slice(i * size, (i + 1) * size)
            rows = jnp.dot(pick_ref[...], block_ref[:, part], preferred_element_type=jnp.float32)
            out_ref[:, part] = (total_ref[:, part] + scale * rows).astype(out_ref.dtype)
            copies.append(pltpu.make_async_copy(out_ref.at[:, part], out_hbm.at[:, part], sems.at[i]))
            copies[-1].start()
        for copy in copies:
            copy.wait()

    return pl.pallas_call(
        kernel,
        out_shape=jax.ShapeDtypeStruct((tok_rows, width), jnp.bfloat16),
        in_specs=[VMEM] * 4,
        out_specs=HBM,
        scratch_shapes=[pltpu.VMEM((tok_rows, width), jnp.bfloat16), pltpu.SemaphoreType.DMA((pieces,))],
        compiler_params=LEAN,
    )(block, total, pick, column)


def per_device(tokens, expert_ids, slot_ids, gate_weights, w_gate, w_up, w_down):
    experts = lax.axis_size("expert")
    rows = lax.axis_size("row")
    cols = lax.axis_size("col")
    capacity = 2 * tokens.shape[0] // experts
    outbound, seat, weight = select(tokens, expert_ids, slot_ids, gate_weights, experts, capacity)
    gate, up, down = bring(w_gate[0], w_up[0], w_down[0])
    returned = []
    for s in range(experts):
        arrived = send(outbound[s], "expert", experts, s) if s else outbound[0]
        blocks = [arrived] + [send(arrived, "row", rows, j) for j in range(1, rows)]
        outgoing, own = enter(blocks, gate, up)
        others = [send(outgoing, "col", cols, j) for j in range(1, cols)]
        term = leave(own, others, down, rows)
        others = [send(term[j], "row", rows, j, True) for j in range(1, rows)]
        total = sum([other.astype(jnp.float32) for other in others], term[0].astype(jnp.float32))
        expert_out = total.astype(jnp.bfloat16)
        returned.append(send(expert_out, "expert", experts, s, True) if s else expert_out)
    order = FINISH if experts == len(FINISH) else tuple(range(experts))
    early, last = order[:-1], order[-1]
    rest = combine_early(early, last, [returned[s] for s in early], seat, weight, tokens.shape[1])
    return combine_last(returned[last], *rest)


def solution(mesh):
    return jax.shard_map(
        per_device,
        mesh=mesh,
        in_specs=(
            P(("group", "expert", "row"), "col"),
            P(("group", "expert", "row"), None),
            P(("group", "expert", "row"), None),
            P(("group", "expert", "row"), None),
            P("expert", "col", "row"),
            P("expert", "col", "row"),
            P("expert", "row", "col"),
        ),
        out_specs=P(("group", "expert", "row"), "col"),
        check_vma=False,
    )
```

```python
import jax
import jax.numpy as jnp
from jax import lax
from jax.experimental import pallas as pl
from jax.experimental.pallas import tpu as pltpu
from jax.sharding import PartitionSpec as P

LEAN = pltpu.CompilerParams(vmem_limit_bytes=8 << 20)
HBM = pl.BlockSpec(memory_space=pltpu.HBM)
VMEM = pl.BlockSpec(memory_space=pltpu.VMEM)
LANES = 128

FINISH = (3, 0, 2, 1)
LATE = 2
GRAY = True


def seat_in_ring(size, index):
    return index ^ (index >> 1) if GRAY and size == 4 else index


def partner(size, step, index):
    return seat_in_ring(size, (seat_in_ring(size, index) + step) % size)


def send(block, axis, size, step, back=False):
    pairs = [(i, partner(size, step, i)) for i in range(size)]
    if back:
        pairs = [(b, a) for a, b in pairs]
    return lax.ppermute(block, axis, pairs)


def step_of(expert_ids, experts):
    mine = seat_in_ring(experts, lax.axis_index("expert"))
    return lax.rem(seat_in_ring(experts, expert_ids) - mine + experts, experts)


def stay(*arrays):
    return [pltpu.with_memory_space_constraint(array, pltpu.HBM) for array in arrays]


def call(kernel, arrays, in_specs, out_shape, scratch=()):
    return pl.pallas_call(
        kernel,
        out_shape=out_shape,
        in_specs=in_specs,
        out_specs=jax.tree.map(lambda _: VMEM, out_shape),
        scratch_shapes=scratch,
        compiler_params=LEAN,
    )(*arrays)


def fetch(pairs, sems):
    copies = [pltpu.make_async_copy(src, dst, sems.at[i]) for i, (src, dst) in enumerate(pairs)]
    for copy in copies:
        copy.start()
    return copies


def select(tokens, expert_ids, slot_ids, gate_weights, experts, capacity):
    tok_rows, width = tokens.shape

    def kernel(ids_hbm, slots_hbm, weights_hbm, tokens_hbm, *refs):
        outs, (seat_ref, weight_ref, ids_ref, slots_ref, weights_ref, tokens_ref, sems) = refs[:experts], refs[experts:]
        copies = fetch(
            ((tokens_hbm, tokens_ref), (ids_hbm, ids_ref), (slots_hbm, slots_ref), (weights_hbm, weights_ref)), sems
        )
        for copy in copies[1:3]:
            copy.wait()
        step = step_of(ids_ref[...], experts)
        slots = slots_ref[...]
        picks = []
        for s in range(experts):
            mine = step == s
            seat = jnp.max(jnp.where(mine, slots, -1), axis=0, keepdims=True)
            seat_ref[s : s + 1, :] = seat
            seats = lax.broadcasted_iota(jnp.int32, (capacity, tok_rows), 0)
            picks.append(jnp.where(seats == seat, 1.0, 0.0).astype(jnp.bfloat16))
        picks = jnp.concatenate(picks, axis=0)
        copies[0].wait()
        rows = jnp.dot(picks, tokens_ref[...], preferred_element_type=jnp.float32)
        for s, out in enumerate(outs):
            out[...] = rows[s * capacity : (s + 1) * capacity].astype(out.dtype)
        copies[3].wait()
        for s in range(experts):
            weight_ref[s : s + 1, :] = jnp.sum(jnp.where(step == s, weights_ref[...], 0.0), axis=0, keepdims=True)

    outs = call(
        kernel,
        stay(expert_ids.T, slot_ids.T, gate_weights.T, tokens),
        [HBM] * 4,
        [pltpu.VMEM((capacity, width), tokens.dtype)] * experts
        + [pltpu.VMEM((experts, tok_rows), jnp.int32), pltpu.VMEM((experts, tok_rows), jnp.float32)],
        [
            pltpu.VMEM((2, tok_rows), jnp.int32),
            pltpu.VMEM((2, tok_rows), jnp.int32),
            pltpu.VMEM((2, tok_rows), jnp.float32),
            pltpu.VMEM((tok_rows, width), tokens.dtype),
            pltpu.SemaphoreType.DMA((4,)),
        ],
    )
    return outs[:experts], outs[experts], outs[experts + 1]


def bring(*arrays):
    def kernel(*refs):
        n = len(arrays)
        for copy in fetch(zip(refs[:n], refs[n : 2 * n]), refs[-1]):
            copy.wait()

    return call(
        kernel,
        stay(*arrays),
        [HBM] * len(arrays),
        [pltpu.VMEM(array.shape, array.dtype) for array in arrays],
        [pltpu.SemaphoreType.DMA((len(arrays),))],
    )


def enter(blocks, gate, up):
    def kernel(*refs):
        *block_refs, gate_ref, up_ref, outgoing_ref, own_ref = refs
        gathered = jnp.concatenate([block[...] for block in block_refs], axis=0)
        cols = gate_ref.shape[1]
        for i, ref in enumerate((gate_ref, up_ref)):
            part = jnp.dot(gathered, ref[...], preferred_element_type=jnp.float32)
            own_ref[:, i * cols : (i + 1) * cols] = part
            outgoing_ref[:, i * cols : (i + 1) * cols] = part.astype(outgoing_ref.dtype)

    shape = (sum(block.shape[0] for block in blocks), 2 * gate.shape[1])
    arrays = (*blocks, gate, up)
    return call(kernel, arrays, [VMEM] * len(arrays), [pltpu.VMEM(shape, jnp.bfloat16), pltpu.VMEM(shape, jnp.float32)])


def leave(own, others, down, rows):
    def kernel(own_ref, *refs):
        summed = own_ref[...]
        cols = summed.shape[1] // 2
        for other in refs[: len(others)]:
            summed = summed + other[...].astype(jnp.float32)
        down_ref, *outs = refs[len(others) :]
        hidden = (jax.nn.silu(summed[:, :cols]) * summed[:, cols:]).astype(jnp.bfloat16)
        term = jnp.dot(hidden, down_ref[...], preferred_element_type=jnp.float32)
        for i, out in enumerate(outs):
            size = out.shape[0]
            out[...] = term[i * size : (i + 1) * size].astype(out.dtype)

    arrays = (own, *others, down)
    shape = (own.shape[0] // rows, down.shape[1])
    return call(kernel, arrays, [VMEM] * len(arrays), [pltpu.VMEM(shape, jnp.bfloat16)] * rows)


def picked(seat_ref, step, capacity):
    seats = lax.broadcasted_iota(jnp.int32, (capacity, seat_ref.shape[1]), 0)
    return jnp.where(seats == seat_ref[step : step + 1, :], 1.0, 0.0)


def combine_early(early, late, blocks, seat, weight):
    tok_rows = seat.shape[1]
    capacity, width = blocks[0].shape

    def kernel(*refs):
        block_refs, (seat_ref, weight_ref, total_ref, *late_refs) = refs[: len(early)], refs[len(early) :]
        columns = jnp.transpose(jnp.concatenate([weight_ref[...]] * -(-8 // weight_ref.shape[0]), axis=0))
        total = 0.0
        for s, block in zip(early, block_refs):
            pick = picked(seat_ref, s, capacity).astype(jnp.bfloat16)
            rows = lax.dot_general(
                pick, block[...], (((0,), (0,)), ((), ())), preferred_element_type=jnp.float32
            )
            total = total + columns[:, s : s + 1] * rows
        total_ref[...] = total
        for s, pick_ref, column_ref in zip(late, late_refs[: len(late)], late_refs[len(late) :]):
            pick_ref[...] = jnp.transpose(picked(seat_ref, s, capacity)).astype(jnp.bfloat16)
            column_ref[...] = jnp.broadcast_to(columns[:, s : s + 1], column_ref.shape)

    arrays = (*blocks, seat, weight)
    return call(
        kernel,
        arrays,
        [VMEM] * len(arrays),
        [pltpu.VMEM((tok_rows, width), jnp.float32)]
        + [pltpu.VMEM((tok_rows, capacity), jnp.bfloat16)] * len(late)
        + [pltpu.VMEM((tok_rows, LANES), jnp.float32)] * len(late),
    )


def combine_late(blocks, total, *late):
    tok_rows, width = total.shape
    n = len(blocks)
    pieces = 2
    size = width // pieces

    def kernel(*refs):
        block_refs, total_ref, pick_refs, column_refs = refs[:n], refs[n], refs[n + 1 : 2 * n + 1], refs[2 * n + 1 : -3]
        out_hbm, out_ref, sems = refs[-3:]
        copies = []
        for i in range(pieces):
            part = slice(i * size, (i + 1) * size)
            result = total_ref[:, part]
            for block, pick, column in zip(block_refs, pick_refs, column_refs):
                rows = jnp.dot(pick[...], block[:, part], preferred_element_type=jnp.float32)
                result = result + jnp.concatenate([column[...]] * (size // LANES), axis=1) * rows
            out_ref[:, part] = result.astype(out_ref.dtype)
            copies.append(pltpu.make_async_copy(out_ref.at[:, part], out_hbm.at[:, part], sems.at[i]))
            copies[-1].start()
        for copy in copies:
            copy.wait()

    arrays = (*blocks, total, *late)
    return pl.pallas_call(
        kernel,
        out_shape=jax.ShapeDtypeStruct((tok_rows, width), jnp.bfloat16),
        in_specs=[VMEM] * len(arrays),
        out_specs=HBM,
        scratch_shapes=[pltpu.VMEM((tok_rows, width), jnp.bfloat16), pltpu.SemaphoreType.DMA((pieces,))],
        compiler_params=LEAN,
    )(*arrays)


def per_device(tokens, expert_ids, slot_ids, gate_weights, w_gate, w_up, w_down):
    experts = lax.axis_size("expert")
    rows = lax.axis_size("row")
    cols = lax.axis_size("col")
    capacity = 2 * tokens.shape[0] // experts
    outbound, seat, weight = select(tokens, expert_ids, slot_ids, gate_weights, experts, capacity)
    gate, up = bring(w_gate[0], w_up[0])
    down = w_down[0]
    returned = []
    for s in range(experts):
        arrived = send(outbound[s], "expert", experts, s) if s else outbound[0]
        blocks = [arrived] + [send(arrived, "row", rows, j) for j in range(1, rows)]
        outgoing, own = enter(blocks, gate, up)
        others = [send(outgoing, "col", cols, j) for j in range(1, cols)]
        term = leave(own, others, down, rows)
        others = [send(term[j], "row", rows, j, True) for j in range(1, rows)]
        total = sum([other.astype(jnp.float32) for other in others], term[0].astype(jnp.float32))
        expert_out = total.astype(jnp.bfloat16)
        returned.append(send(expert_out, "expert", experts, s, True) if s else expert_out)
    order = FINISH if experts == len(FINISH) else tuple(range(experts))
    early, late = order[:-LATE], order[-LATE:]
    rest = combine_early(early, late, [returned[s] for s in early], seat, weight)
    return combine_late([returned[s] for s in late], *rest)


def solution(mesh):
    return jax.shard_map(
        per_device,
        mesh=mesh,
        in_specs=(
            P(("group", "expert", "row"), "col"),
            P(("group", "expert", "row"), None),
            P(("group", "expert", "row"), None),
            P(("group", "expert", "row"), None),
            P("expert", "col", "row"),
            P("expert", "col", "row"),
            P("expert", "row", "col"),
        ),
        out_specs=P(("group", "expert", "row"), "col"),
        check_vma=False,
    )
```
